128 devices in a mesh: hid: 32 (over x_lo, z, y), dp: 4 (over x_hi, core).
Axes of the slice: x: 4 (x_hi: 2, x_lo: 2; x = x_hi * 2 + x_lo), y: 4, z: 4, core: 2. Of those that a mesh axis runs over, the one named last changes fastest.
Arguments:
- hidden_acts: bfloat16 [1024, 65536], P('dp', 'hid'), may hold values from -6 to 6
- out_grads: bfloat16 [1024, 1024], P('dp'), may hold values from -6 to 6
- damping: float32 [64], replicated, may hold values from 0.05 to 1
Outputs:
- update: bfloat16 [65536, 1024], P('hid')
The draws below stay inside these ranges and needn't reach their ends.
All inputs are finite; a program needn't handle non-finite values.
Results may differ from the reference program's by a relative error of at most 0.0023.
Values may be sent and summed in bfloat16 or wider, within the bound.
A program may use at most 128 MiB of HBM per device.

```python
import math
import jax
import jax.numpy as jnp
from jax import lax

D = 1024
FF = 65536
BLOCK = 1024
ITERS = 3
TOKENS = 1024
BLOCKS = 64


def level_of(own_key, shape, pieces, least, top_value):
    def one(position, blocks):
        heights = jax.random.uniform(jax.random.fold_in(jax.random.fold_in(own_key, 6), position), (blocks,), jnp.float32, least / len(pieces), top_value / len(pieces))
        return jnp.repeat(jnp.exp(heights), shape[position] // blocks).reshape((-1,) + (1,) * (len(shape) - position - 1))

    level = one(*pieces[0])
    for cut in pieces[1:]:
        level = level * one(*cut)
    return level


def centred(stream_key, extent, width, limit, pieces=(), held_as=jnp.bfloat16):
    array = width * jax.random.normal(stream_key, extent, jnp.float32)
    if pieces:
        array = array * level_of(stream_key, extent, pieces, -0.22, 0.18)
    return jnp.clip(array, -limit, limit).astype(held_as)


def setup_inputs(seed: int = 0) -> dict:
    seeds = jax.random.split(jax.random.key(seed), 4)
    hidden_acts = centred(seeds[0], (TOKENS, FF), 1.0, 6.0, ((0, 4), (1, 32)))
    out_grads = centred(seeds[1], (TOKENS, D), 1.0, 6.0, ((0, 4),))
    damping = jnp.clip(jnp.exp(jax.random.uniform(seeds[2], (BLOCKS,), jnp.float32, math.log(0.05), math.log(1.0))), 0.05, 1.0)
    return {"hidden_acts": hidden_acts, "out_grads": out_grads, "damping": damping}


out_damping = 0.1

def newton(matrix):
    order = matrix.shape[0]
    start_scale = 1.0 / jnp.sqrt(jnp.sum(matrix * matrix))
    inverse = start_scale * jnp.eye(order, dtype=jnp.float32)
    for iteration in range(ITERS):
        product = jnp.dot(matrix, inverse, precision=lax.Precision.HIGHEST)
        product = jnp.dot(product, inverse, precision=lax.Precision.HIGHEST)
        inverse = 2.0 * inverse - product
    return inverse

def reference(hidden_acts, out_grads, damping):
    out_factor = jnp.dot(out_grads.T, out_grads, preferred_element_type=jnp.float32) / TOKENS
    out_factor = out_factor + out_damping * jnp.eye(D, dtype=jnp.float32)
    out_inverse = newton(out_factor)
    hidden_blocks = hidden_acts.reshape(TOKENS, BLOCKS, BLOCK).transpose(1, 0, 2)

    def per_block(inputs):
        columns, block_damping = inputs
        in_factor = jnp.dot(columns.T, columns, preferred_element_type=jnp.float32) / TOKENS
        in_factor = in_factor + block_damping * jnp.eye(BLOCK, dtype=jnp.float32)
        in_inverse = newton(in_factor)
        grad = jnp.dot(columns.T, out_grads, preferred_element_type=jnp.float32)
        right = jnp.dot(grad, out_inverse, precision=lax.Precision.HIGHEST)
        return jnp.dot(in_inverse, right, precision=lax.Precision.HIGHEST).astype(jnp.bfloat16)
    result = lax.map(per_block, (hidden_blocks, damping))
    return result.reshape(FF, D)
```

```python
import functools

import jax
import jax.numpy as jnp
from jax import lax
from jax.experimental import pallas as pl
from jax.experimental.pallas import tpu as pltpu
from jax.sharding import PartitionSpec as P

BLOCK = 1024
TILE = 512
OUT_DAMPING = 0.1
F32, BF16 = jnp.float32, jnp.bfloat16
MESH = pl.DeviceIdType.MESH
TOKENS_FIRST = (((0,), (0,)), ((), ()))

STAGE0, G_SIB, H_SIB, H_FAR, H_FARX = 0, 1, 2, 3, 4
STAGE1, STAGE2, FORWARD, CORR, RESULT = 5, 8, 11, 15, 17
OUT_TILES = 4
N_REMOTE = RESULT + OUT_TILES


def mm(a, b):
    return jnp.dot(a, b, preferred_element_type=F32)


def mmt(a, b):
    return lax.dot_general(a, b, TOKENS_FIRST, preferred_element_type=F32)


def tiles(count, size, body):
    def step(j, carry):
        body(j, pl.ds(pl.multiple_of(j * size, size), size))
        return carry

    lax.fori_loop(0, count, step, 0)


def kernel(h_hbm, g_hbm, damping, o_hbm, h, g, mo, mob, p2, p2b, p4b, cf, zb, zc,
           mi, y, ya, yb, part, send, recv, here):
    tok = h_hbm.shape[0]
    hid, dp = lax.axis_index("hid"), lax.axis_index("dp")
    xlo, zc_, yc_ = hid // 16, (hid // 4) % 4, hid % 4
    xhi, core = dp // 2, dp % 2

    first = yc_ + core * (zc_ - yc_)
    second = zc_ + core * (yc_ - zc_)

    def plane(move_first, move_second):
        f, s = (first + move_first) % 4, (second + move_second) % 4
        ny = f + core * (s - f)
        nz = s + core * (f - s)
        return (xlo * 16 + nz * 4 + ny, dp)

    sibling = (hid, xhi * 2 + 1 - core)
    far = (hid, (1 - xhi) * 2 + core)
    farx = (hid, (1 - xhi) * 2 + 1 - core)
    cut = ((1 - xlo) * 16 + zc_ * 4 + yc_, (1 - xhi) * 2 + core)
    firsts = [plane(i, 0) for i in range(1, 4)]
    seconds = [plane(0, i) for i in range(1, 4)]

    barrier = pltpu.get_barrier_semaphore()
    partners = [sibling, far, farx, cut] + firsts + seconds
    for partner in partners:
        pl.semaphore_signal(barrier, 1, device_id=partner, device_id_type=MESH)
    pl.semaphore_wait(barrier, len(partners))

    def remote(src, dst, slot, device):
        return pltpu.make_async_remote_copy(
            src_ref=src, dst_ref=dst, send_sem=send.at[slot], recv_sem=recv.at[slot],
            device_id=device, device_id_type=MESH)

    def slot(i):
        return pl.ds(i * tok, tok)

    def g_rows(base, start, size):
        return g.at[pl.ds(pl.multiple_of(base * tok + start, 16), size)]

    own_cols = pl.ds(pl.multiple_of(core * BLOCK, BLOCK), BLOCK)
    other_cols = pl.ds(pl.multiple_of((1 - core) * BLOCK, BLOCK), BLOCK)
    piece, group = tok // 16, tok // 4
    own_piece = (second * 4 + first) * piece

    stage0 = remote(g_hbm.at[pl.ds(pl.multiple_of(own_piece, 16), piece)],
                    g_rows(2, own_piece, piece), STAGE0, cut)
    stage0.start()
    g_own = pltpu.make_async_copy(g_hbm, g.at[slot(0)], here.at[0])
    g_own.start()
    g_sib = remote(g_hbm, g.at[slot(1)], G_SIB, sibling)
    g_sib.start()
    h_own = pltpu.make_async_copy(h_hbm.at[:, own_cols], h.at[slot(0)], here.at[1])
    h_own.start()
    h_sib = remote(h_hbm.at[:, other_cols], h.at[slot(1)], H_SIB, sibling)
    h_sib.start()
    h_far = remote(h_hbm.at[:, own_cols], h.at[slot(2)], H_FAR, far)
    h_far.start()
    h_farx = remote(h_hbm.at[:, other_cols], h.at[slot(3)], H_FARX, farx)
    h_farx.start()

    stage0.wait_recv()
    stage1 = [remote(g_rows(2, own_piece, piece), g_rows(2, own_piece, piece),
                     STAGE1 + i, firsts[i]) for i in range(3)]
    for copy in stage1:
        copy.start()

    g_own.wait()
    g_sib.wait_recv()

    def out_local(j, rs):
        mo[rs, :] = mmt(g[0:2 * tok, rs], g[0:2 * tok, :])

    tiles(2, TILE, out_local)

    for i in range(3):
        came = (second * 4 + (first + 3 - i) % 4) * piece
        remote(g_rows(2, came, piece), g_rows(2, came, piece), STAGE1 + i, firsts[i]).wait_recv()
    own_group = second * group
    stage2 = [remote(g_rows(2, own_group, group), g_rows(2, own_group, group),
                     STAGE2 + i, seconds[i]) for i in range(3)]
    for copy in stage2:
        copy.start()
    forwards = [remote(g_rows(2, own_group, group), g_rows(3, own_group, group), FORWARD, sibling)]
    forwards[0].start()

    h_own.wait()
    h_sib.wait_recv()

    def in_local(j, rs):
        mi[rs, :] = mmt(h[0:2 * tok, rs], h[0:2 * tok, :])
        y[rs, :] = mmt(h[0:2 * tok, rs], g[0:2 * tok, :])

    tiles(2, TILE, in_local)

    for i in range(3):
        came = ((second + 3 - i) % 4) * group
        remote(g_rows(2, came, group), g_rows(2, came, group), STAGE2 + i, seconds[i]).wait_recv()
        forward = remote(g_rows(2, came, group), g_rows(3, came, group), FORWARD + 1 + i, sibling)
        forward.start()
        forwards.append(forward)
    for i in range(4):
        came = ((first + 4 - i) % 4) * group
        remote(g_rows(3, came, group), g_rows(3, came, group), FORWARD + i, sibling).wait_recv()

    def ridge(j, size, amount):
        row = lax.broadcasted_iota(jnp.int32, (size, BLOCK), 0) + j * size
        col = lax.broadcasted_iota(jnp.int32, (size, BLOCK), 1)
        return jnp.where(row == col, amount, 0.0)

    def add_squares(j, m):
        squares = jnp.sum((m * m).reshape(TILE // 8, 8, BLOCK), axis=0)

        @pl.when(j == 0)
        def _():
            part[...] = squares

        @pl.when(j > 0)
        def _():
            part[...] += squares

    def scale():
        return 1.0 / jnp.sqrt(jnp.sum(part[...], keepdims=True))

    scale_tokens = 1.0 / (4 * tok)

    def out_factor(j, rs):
        m = mo[rs, :] + mmt(g[2 * tok:4 * tok, rs], g[2 * tok:4 * tok, :])
        m = m * scale_tokens + ridge(j, TILE, OUT_DAMPING)
        mo[rs, :] = m
        mob[rs, :] = m.astype(BF16)
        add_squares(j, m)

    tiles(2, TILE, out_factor)
    so = scale()

    def out_two(j, rs):
        n2 = (2.0 * so) * mo[rs, :] - (so * so) * mm(mob[rs, :], mob[...])
        p2[rs, :] = n2
        p2b[rs, :] = n2.astype(BF16)

    tiles(2, TILE, out_two)

    def mine(j):
        return pl.ds(pl.multiple_of(j * 2 * tok, tok), tok)

    def corr_one(j, rs):
        c1 = so * mm(g[mine(j), :], mob[...])
        cf[rs, :] = c1
        zb[rs, :] = (2.0 * g[mine(j), :].astype(F32) - c1).astype(BF16)

    tiles(2, tok, corr_one)

    def out_four(j, rs):
        n4 = 2.0 * p2[rs, :] - mm(p2b[rs, :], p2b[...])
        p4b[rs, :] = n4.astype(BF16)

    tiles(2, TILE, out_four)

    def corr_two(j, rs):
        c2 = 2.0 * cf[rs, :] + mm(zb[rs, :], p2b[...])
        cf[rs, :] = c2
        zb[rs, :] = (4.0 * g[mine(j), :].astype(F32) - c2).astype(BF16)

    tiles(2, tok, corr_two)

    def corr_three(j, rs):
        c3 = 2.0 * cf[rs, :] + mm(zb[rs, :], p4b[...])
        zc[mine(j), :] = (c3 * -0.125).astype(BF16)

    tiles(2, tok, corr_three)
    corr = [remote(zc.at[slot(2 * i)], zc.at[slot(2 * i + 1)], CORR + i, sibling) for i in range(2)]
    for copy in corr:
        copy.start()

    h_far.wait_recv()

    def in_far(j, rs):
        mi[rs, :] += mmt(h[2 * tok:3 * tok, rs], h[2 * tok:3 * tok, :])

    tiles(2, TILE, in_far)
    for copy in corr:
        copy.wait_recv()

    def right_far(j, rs):
        y[rs, :] += (mmt(h[2 * tok:3 * tok, rs], g[2 * tok:3 * tok, :])
                     + mmt(h[0:3 * tok, rs], zc[0:3 * tok, :]))

    tiles(2, TILE, right_far)

    h_farx.wait_recv()
    block_damping = damping[hid * 2 + core]

    def in_factor(j, rs):
        m = mi[rs, :] + mmt(h[3 * tok:4 * tok, rs], h[3 * tok:4 * tok, :])
        m = m * scale_tokens + ridge(j, TILE, block_damping)
        mi[rs, :] = m
        mob[rs, :] = m.astype(BF16)
        add_squares(j, m)

    tiles(2, TILE, in_factor)
    si = scale()

    def right_last(j, rs):
        r = (y[rs, :] + mmt(h[3 * tok:4 * tok, rs], g[3 * tok:4 * tok, :])
             + mmt(h[3 * tok:4 * tok, rs], zc[3 * tok:4 * tok, :]))
        y[rs, :] = r
        ya[rs, :] = r.astype(BF16)

    tiles(2, TILE, right_last)

    def in_two(j, rs):
        n2 = (2.0 * si) * mi[rs, :] - (si * si) * mm(mob[rs, :], mob[...])
        p2[rs, :] = n2
        p2b[rs, :] = n2.astype(BF16)

    tiles(2, TILE, in_two)

    def apply_one(j, rs):
        r = 2.0 * y[rs, :] - si * mm(mob[rs, :], ya[...])
        y[rs, :] = r
        yb[rs, :] = r.astype(BF16)

    tiles(2, TILE, apply_one)

    def in_four(j, rs):
        n4 = 2.0 * p2[rs, :] - mm(p2b[rs, :], p2b[...])
        p4b[rs, :] = n4.astype(BF16)

    tiles(2, TILE, in_four)

    def apply_two(j, rs):
        r = 2.0 * y[rs, :] - mm(p2b[rs, :], yb[...])
        y[rs, :] = r
        ya[rs, :] = r.astype(BF16)

    tiles(2, TILE, apply_two)

    final = 8.0 * si * so
    span = BLOCK // OUT_TILES

    def out_copies(j):
        src = yb.at[pl.ds(pl.multiple_of(j * span, span), span)]
        dst = o_hbm.at[pl.ds(pl.multiple_of(core * BLOCK + j * span, span), span)]
        return (pltpu.make_async_copy(src, dst, here.at[2 + j]),
                remote(src, dst, RESULT + j, sibling))

    def apply_three(j, rs):
        r = 2.0 * y[rs, :] - mm(p4b[rs, :], ya[...])
        yb[rs, :] = (final * r).astype(BF16)
        for copy in out_copies(j):
            copy.start()

    tiles(OUT_TILES, span, apply_three)

    for copy in [stage0, g_sib, h_sib, h_far, h_farx] + stage1 + stage2 + forwards + corr:
        copy.wait_send()
    for j in range(OUT_TILES):
        local_copy, far_copy = out_copies(j)
        local_copy.wait()
        far_copy.wait_send()
        src = yb.at[pl.ds(j * span, span)]
        dst = o_hbm.at[pl.ds(pl.multiple_of((1 - core) * BLOCK + j * span, span), span)]
        remote(src, dst, RESULT + j, sibling).wait_recv()


def local(hidden_acts, out_grads, damping):
    tok, width = hidden_acts.shape
    square = (BLOCK, BLOCK)
    hbm = pl.BlockSpec(memory_space=pl.ANY)
    return pl.pallas_call(
        kernel,
        name="kfac_step",
        out_shape=jax.ShapeDtypeStruct((width, BLOCK), BF16),
        in_specs=[hbm, hbm, pl.BlockSpec(memory_space=pltpu.SMEM)],
        out_specs=hbm,
        scratch_shapes=[
            pltpu.VMEM(square, BF16),
            pltpu.VMEM(square, BF16),
            pltpu.VMEM(square, F32),
            pltpu.VMEM(square, BF16),
            pltpu.VMEM(square, F32),
            pltpu.VMEM(square, BF16),
            pltpu.VMEM(square, BF16),
            pltpu.VMEM((BLOCK // 2, BLOCK), F32),
            pltpu.VMEM((BLOCK // 2, BLOCK), BF16),
            pltpu.VMEM(square, BF16),
            pltpu.VMEM(square, F32),
            pltpu.VMEM(square, F32),
            pltpu.VMEM(square, BF16),
            pltpu.VMEM(square, BF16),
            pltpu.VMEM((8, BLOCK), F32),
            pltpu.SemaphoreType.DMA((N_REMOTE,)),
            pltpu.SemaphoreType.DMA((N_REMOTE,)),
            pltpu.SemaphoreType.DMA((2 + OUT_TILES,)),
        ],
        compiler_params=pltpu.CompilerParams(
            collective_id=0, has_side_effects=True, vmem_limit_bytes=56 << 20
        ),
    )(hidden_acts, out_grads, damping)


def solution(mesh):
    return jax.shard_map(
        local,
        mesh=mesh,
        in_specs=(P("dp", "hid"), P("dp", None), P()),
        out_specs=P("hid", None),
        check_vma=False,
    )
```

```python
import jax
import jax.numpy as jnp
from jax import lax
from jax.experimental import pallas as pl
from jax.experimental.pallas import tpu as pltpu
from jax.sharding import PartitionSpec as P

BLOCK = 1024
OUT_DAMPING = 0.1
F32, BF16 = jnp.float32, jnp.bfloat16
MESH = pl.DeviceIdType.MESH
TOKENS_FIRST = (((0,), (0,)), ((), ()))

TOK = 256
GROUP = TOK // 4
PIECE = TOK // 16
PARTS = 8
PART = TOK // PARTS
ISSUE = (0, 0, 8, 8)
LATE = 3 * GROUP * 2
OUT_TILES = 4

STAGE0, G_SIB, H_SIB = 0, 1, 2
STAGE1, STAGE2, FORWARD, CORR = 3, 6, 9, 13
RESULT = 18
H_FAR = RESULT + OUT_TILES
H_FARX = H_FAR + PARTS
N_REMOTE = H_FARX + PARTS


def mm(a, b):
    return jnp.dot(a, b, preferred_element_type=F32)


def mmt(a, b):
    return lax.dot_general(a, b, TOKENS_FIRST, preferred_element_type=F32)


def total(m):
    rows = m.shape[0]
    return jnp.sum(jnp.sum((m * m).reshape(rows // 8, 8, BLOCK), axis=0), keepdims=True)


def ridge(amount):
    row = lax.broadcasted_iota(jnp.int32, (BLOCK, BLOCK), 0)
    col = lax.broadcasted_iota(jnp.int32, (BLOCK, BLOCK), 1)
    return jnp.where(row == col, amount, 0.0)


def step(body):
    body()


def kernel(h_hbm, g_hbm, damping, o_hbm, h, g, mo, mob, p2, p2b, p4b, cf, zb, zc,
           mi, y, ya, yb, send, recv, here):
    hid, dp = lax.axis_index("hid"), lax.axis_index("dp")
    xlo, zpos, ypos = hid // 16, (hid // 4) % 4, hid % 4
    xhi, core = dp // 2, dp % 2

    first = ypos + core * (zpos - ypos)
    second = zpos + core * (ypos - zpos)

    def plane(move_first, move_second):
        f, s = (first + move_first) % 4, (second + move_second) % 4
        ny = f + core * (s - f)
        nz = s + core * (f - s)
        return (xlo * 16 + nz * 4 + ny, dp)

    sibling = (hid, xhi * 2 + 1 - core)
    far = (hid, (1 - xhi) * 2 + core)
    farx = (hid, (1 - xhi) * 2 + 1 - core)
    cut = ((1 - xlo) * 16 + zpos * 4 + ypos, (1 - xhi) * 2 + core)
    firsts = [plane(i, 0) for i in range(1, 4)]
    seconds = [plane(0, i) for i in range(1, 4)]

    barrier = pltpu.get_barrier_semaphore()
    partners = [sibling, far, farx, cut] + firsts + seconds
    for partner in partners:
        pl.semaphore_signal(barrier, 1, device_id=partner, device_id_type=MESH)
    pl.semaphore_wait(barrier, len(partners))

    def remote(src, dst, slot, device):
        return pltpu.make_async_remote_copy(
            src_ref=src, dst_ref=dst, send_sem=send.at[slot], recv_sem=recv.at[slot],
            device_id=device, device_id_type=MESH)

    def far_row(side, group):
        return 2 * TOK + group * (2 * GROUP) + side * GROUP

    def g_piece(group, piece):
        return g.at[pl.ds(pl.multiple_of(far_row(0, group) + piece * PIECE, 16), PIECE)]

    def g_group(side, group):
        return g.at[pl.ds(pl.multiple_of(far_row(side, group), 16), GROUP)]

    own_cols = pl.ds(pl.multiple_of(core * BLOCK, BLOCK), BLOCK)
    other_cols = pl.ds(pl.multiple_of((1 - core) * BLOCK, BLOCK), BLOCK)

    h_sent = []

    def send_far(count):
        while len(h_sent) < 2 * count:
            part = len(h_sent) // 2
            rows = pl.ds(part * PART, PART)
            group, inside = part * PART // GROUP, part * PART % GROUP
            to_far = remote(h_hbm.at[rows, own_cols],
                            h.at[pl.ds(far_row(0, group) + inside, PART)], H_FAR + part, far)
            to_farx = remote(h_hbm.at[rows, other_cols],
                             h.at[pl.ds(far_row(1, group) + inside, PART)], H_FARX + part, farx)
            to_far.start()
            to_farx.start()
            h_sent.extend([to_far, to_farx])

    stage0 = remote(g_hbm.at[pl.ds(pl.multiple_of((second * 4 + first) * PIECE, 16), PIECE)],
                    g_piece(second, first), STAGE0, cut)
    stage0.start()
    g_own = pltpu.make_async_copy(g_hbm, g.at[pl.ds(0, TOK)], here.at[0])
    g_own.start()
    g_sib = remote(g_hbm, g.at[pl.ds(TOK, TOK)], G_SIB, sibling)
    g_sib.start()
    send_far(ISSUE[0])
    h_own = pltpu.make_async_copy(h_hbm.at[:, own_cols], h.at[pl.ds(0, TOK)], here.at[1])
    h_own.start()
    h_sib = remote(h_hbm.at[:, other_cols], h.at[pl.ds(TOK, TOK)], H_SIB, sibling)
    h_sib.start()

    stage0.wait_recv()
    stage1 = [remote(g_piece(second, first), g_piece(second, first), STAGE1 + i, firsts[i])
              for i in range(3)]
    for copy in stage1:
        copy.start()
    send_far(ISSUE[1])

    near = slice(0, 2 * TOK)
    rest = slice(2 * TOK, 4 * TOK)
    early = slice(2 * TOK, 2 * TOK + LATE)
    last = slice(2 * TOK + LATE, 4 * TOK)

    g_own.wait()
    g_sib.wait_recv()

    @step
    def out_local():
        mo[...] = mmt(g[near, :], g[near, :])

    for i in range(3):
        came = g_piece(second, (first + 3 - i) % 4)
        remote(came, came, STAGE1 + i, firsts[i]).wait_recv()
    stage2 = [remote(g_group(0, second), g_group(0, second), STAGE2 + i, seconds[i])
              for i in range(3)]
    for copy in stage2:
        copy.start()
    forwards = [remote(g_group(0, second), g_group(1, second), FORWARD, sibling)]
    forwards[0].start()
    send_far(ISSUE[2])

    h_own.wait()
    h_sib.wait_recv()

    @step
    def in_local():
        mi[...] = mmt(h[near, :], h[near, :])
        y[...] = mmt(h[near, :], g[near, :])

    for i in range(3):
        group = (second + 3 - i) % 4
        remote(g_group(0, group), g_group(0, group), STAGE2 + i, seconds[i]).wait_recv()
        forward = remote(g_group(0, group), g_group(1, group), FORWARD + 1 + i, sibling)
        forward.start()
        forwards.append(forward)
    send_far(ISSUE[3])
    for i in range(4):
        group = (first + 4 - i) % 4
        remote(g_group(1, group), g_group(1, group), FORWARD + i, sibling).wait_recv()

    scale_tokens = 1.0 / (4 * TOK)

    @step
    def out_factor():
        m = (mo[...] + mmt(g[rest, :], g[rest, :])) * scale_tokens + ridge(OUT_DAMPING)
        mo[...] = m
        mob[...] = m.astype(BF16)

    so = 1.0 / jnp.sqrt(total(mo[...]))

    mine = [(0, TOK)] + [(far_row(0, k), GROUP) for k in range(4)]

    def packed(ref):
        return jnp.concatenate([ref[a:a + n, :] for a, n in mine], axis=0)

    @step
    def out_two():
        n2 = (2.0 * so) * mo[...] - (so * so) * mm(mob[...], mob[...])
        p2[...] = n2
        p2b[...] = n2.astype(BF16)

    @step
    def corr_one():
        gm = packed(g)
        c1 = so * mm(gm, mob[...])
        cf[...] = c1
        zb[...] = (2.0 * gm.astype(F32) - c1).astype(BF16)

    @step
    def out_four():
        n4 = 2.0 * p2[...] - mm(p2b[...], p2b[...])
        p4b[...] = n4.astype(BF16)

    @step
    def corr_two():
        c2 = 2.0 * cf[...] + mm(zb[...], p2b[...])
        cf[...] = c2
        zb[...] = (4.0 * packed(g).astype(F32) - c2).astype(BF16)

    corr = []

    @step
    def corr_three():
        c3 = ((2.0 * cf[...] + mm(zb[...], p4b[...])) * -0.125).astype(BF16)
        at = 0
        for a, n in mine:
            zc[a:a + n, :] = c3[at:at + n, :]
            at += n

    for i, (a, n) in enumerate(mine):
        copy = remote(zc.at[pl.ds(a, n)], zc.at[pl.ds(a + n, n)], CORR + i, sibling)
        copy.start()
        corr.append(copy)

    def take_far(lo, hi):
        for part in range(lo, hi):
            h_sent[2 * part].wait_recv()
            h_sent[2 * part + 1].wait_recv()

    early_parts = LATE // (2 * PART)
    take_far(0, early_parts)

    @step
    def in_early():
        mi[...] += mmt(h[early, :], h[early, :])
        y[...] += mmt(h[early, :], g[early, :])

    for copy in corr:
        copy.wait_recv()

    @step
    def right_early():
        y[...] += mmt(h[0:2 * TOK + LATE, :], zc[0:2 * TOK + LATE, :])

    take_far(early_parts, PARTS)
    block_damping = damping[hid * 2 + core]

    @step
    def in_factor():
        m = (mi[...] + mmt(h[last, :], h[last, :])) * scale_tokens + ridge(block_damping)
        mi[...] = m
        mob[...] = m.astype(BF16)

    si = 1.0 / jnp.sqrt(total(mi[...]))

    @step
    def right_last():
        r = y[...] + mmt(h[last, :], g[last, :]) + mmt(h[last, :], zc[last, :])
        y[...] = r
        ya[...] = r.astype(BF16)

    @step
    def in_two():
        n2 = (2.0 * si) * mi[...] - (si * si) * mm(mob[...], mob[...])
        p2[...] = n2
        p2b[...] = n2.astype(BF16)

    @step
    def apply_one():
        r = 2.0 * y[...] - si * mm(mob[...], ya[...])
        y[...] = r
        yb[...] = r.astype(BF16)

    @step
    def in_four():
        n4 = 2.0 * p2[...] - mm(p2b[...], p2b[...])
        p4b[...] = n4.astype(BF16)

    @step
    def apply_two():
        r = 2.0 * y[...] - mm(p2b[...], yb[...])
        y[...] = r
        ya[...] = r.astype(BF16)

    final = 8.0 * si * so
    span = BLOCK // OUT_TILES

    def out_copies(j):
        src = yb.at[pl.ds(j * span, span)]
        dst = o_hbm.at[pl.ds(pl.multiple_of(core * BLOCK + j * span, span), span)]
        return (pltpu.make_async_copy(src, dst, here.at[2 + j]),
                remote(src, dst, RESULT + j, sibling))

    results = []
    for j in range(OUT_TILES):
        rs = slice(j * span, (j + 1) * span)

        @step
        def apply_three():
            r = 2.0 * y[rs, :] - mm(p4b[rs, :], ya[...])
            yb[rs, :] = (final * r).astype(BF16)

        copies = out_copies(j)
        for copy in copies:
            copy.start()
        results.append(copies)

    for copy in [stage0, g_sib, h_sib] + h_sent + stage1 + stage2 + forwards + corr:
        copy.wait_send()
    for j, (local_copy, far_copy) in enumerate(results):
        local_copy.wait()
        far_copy.wait_send()
        src = yb.at[pl.ds(j * span, span)]
        dst = o_hbm.at[pl.ds(pl.multiple_of((1 - core) * BLOCK + j * span, span), span)]
        remote(src, dst, RESULT + j, sibling).wait_recv()


def local(hidden_acts, out_grads, damping):
    width = hidden_acts.shape[1]
    square = (BLOCK, BLOCK)
    hbm = pl.BlockSpec(memory_space=pl.ANY)
    return pl.pallas_call(
        kernel,
        name="kfac_step",
        out_shape=jax.ShapeDtypeStruct((width, BLOCK), BF16),
        in_specs=[hbm, hbm, pl.BlockSpec(memory_space=pltpu.SMEM)],
        out_specs=hbm,
        scratch_shapes=[
            pltpu.VMEM(square, BF16),
            pltpu.VMEM(square, BF16),
            pltpu.VMEM(square, F32),
            pltpu.VMEM(square, BF16),
            pltpu.VMEM(square, F32),
            pltpu.VMEM(square, BF16),
            pltpu.VMEM(square, BF16),
            pltpu.VMEM((BLOCK // 2, BLOCK), F32),
            pltpu.VMEM((BLOCK // 2, BLOCK), BF16),
            pltpu.VMEM(square, BF16),
            pltpu.VMEM(square, F32),
            pltpu.VMEM(square, F32),
            pltpu.VMEM(square, BF16),
            pltpu.VMEM(square, BF16),
            pltpu.SemaphoreType.DMA((N_REMOTE,)),
            pltpu.SemaphoreType.DMA((N_REMOTE,)),
            pltpu.SemaphoreType.DMA((2 + OUT_TILES,)),
        ],
        compiler_params=pltpu.CompilerParams(
            collective_id=0, has_side_effects=True, vmem_limit_bytes=56 << 20
        ),
    )(hidden_acts, out_grads, damping)


def solution(mesh):
    return jax.shard_map(
        local,
        mesh=mesh,
        in_specs=(P("dp", "hid"), P("dp", None), P()),
        out_specs=P("hid", None),
        check_vma=False,
    )
```

```python
import jax
import jax.numpy as jnp
from jax import lax
from jax.experimental import pallas as pl
from jax.experimental.pallas import tpu as pltpu
from jax.sharding import PartitionSpec as P

BLOCK = 1024
OUT_DAMPING = 0.1
F32, BF16 = jnp.float32, jnp.bfloat16
MESH = pl.DeviceIdType.MESH
TOKENS_FIRST = (((0,), (0,)), ((), ()))

HALF = BLOCK // 2
TOP, LOW = slice(0, HALF), slice(HALF, BLOCK)

TOK = 256
GROUP = TOK // 4
START_PARTS = 0
PARTS = 8
PART = TOK // PARTS
LATE = 3 * GROUP * 2
OUT_TILES = 4

STAGE0, G_SIB, H_SIB, STAGE1, FORWARD, CORR, RESULT = 0, 1, 2, 3, 6, 10, 15
H_FAR = RESULT + OUT_TILES
H_FARX = H_FAR + PARTS
N_REMOTE = H_FARX + PARTS


def mm(a, b):
    return jnp.dot(a, b, preferred_element_type=F32)


def mmt(a, b):
    return lax.dot_general(a, b, TOKENS_FIRST, preferred_element_type=F32)


def total(m):
    rows, cols = m.shape
    return jnp.sum(jnp.sum((m * m).reshape(rows // 8, 8, cols), axis=0), keepdims=True)


def ridge(rows, cols, amount):
    row = lax.broadcasted_iota(jnp.int32, (rows, cols), 0)
    col = lax.broadcasted_iota(jnp.int32, (rows, cols), 1)
    return jnp.where(row == col, amount, 0.0)


def keep(ref, top, low):
    ref[TOP, :] = top
    ref[LOW, LOW] = low


def keep_whole(ref, top, low):
    keep(ref, top.astype(BF16), low.astype(BF16))
    ref[LOW, TOP] = top[:, LOW].astype(BF16).T


def gram(a):
    return mmt(a[:, TOP], a), mmt(a[:, LOW], a[:, LOW])


def add_gram(ref, a):
    top, low = gram(a)
    keep(ref, ref[TOP, :] + top, ref[LOW, LOW] + low)


def factor(ref, whole, a, scale, amount):
    top, low = gram(a)
    top = (ref[TOP, :] + top) * scale + ridge(HALF, BLOCK, amount)
    low = (ref[LOW, LOW] + low) * scale + ridge(HALF, HALF, amount)
    keep(ref, top, low)
    keep_whole(whole, top, low)
    return total(top[:, TOP]) + 2.0 * total(top[:, LOW]) + total(low)


def residual(ref, whole, linear, square):
    return (linear * ref[TOP, :] - square * mm(whole[TOP, :], whole[...]),
            linear * ref[LOW, LOW] - square * mm(whole[LOW, :], whole[:, LOW]))


def step(body):
    body()


def kernel(h_hbm, g_hbm, damping_hbm, u, h, g, mo, mob, p2, p2b, p4b, cf, zb, zc,
           mi, y, ya, yb, damping, send, recv, here):
    hid, dp = lax.axis_index("hid"), lax.axis_index("dp")
    xlo, zpos, ypos = hid // 16, (hid // 4) % 4, hid % 4
    xhi, core = dp // 2, dp % 2

    place = ypos + core * (zpos - ypos)

    def beside(move):
        ny = ypos + (1 - core) * ((ypos + move) % 4 - ypos)
        nz = zpos + core * ((zpos + move) % 4 - zpos)
        return (xlo * 16 + nz * 4 + ny, dp)

    sibling = (hid, xhi * 2 + 1 - core)
    far = (hid, (1 - xhi) * 2 + core)
    farx = (hid, (1 - xhi) * 2 + 1 - core)
    cut = ((1 - xlo) * 16 + zpos * 4 + ypos, (1 - xhi) * 2 + core)
    line = [beside(i) for i in range(1, 4)]

    own_cols = pl.ds(pl.multiple_of(core * BLOCK, BLOCK), BLOCK)
    other_cols = pl.ds(pl.multiple_of((1 - core) * BLOCK, BLOCK), BLOCK)
    g_own = pltpu.make_async_copy(g_hbm, g.at[pl.ds(0, TOK)], here.at[0])
    g_own.start()
    h_own = pltpu.make_async_copy(h_hbm.at[:, own_cols], h.at[pl.ds(0, TOK)], here.at[1])
    h_own.start()

    damping_own = pltpu.make_async_copy(damping_hbm, damping, here.at[2])
    damping_own.start()

    barrier = pltpu.get_barrier_semaphore()
    partners = [sibling, far, farx, cut] + line
    for partner in partners:
        pl.semaphore_signal(barrier, 1, device_id=partner, device_id_type=MESH)
    pl.semaphore_wait(barrier, len(partners))

    def remote(src, dst, slot, device):
        return pltpu.make_async_remote_copy(
            src_ref=src, dst_ref=dst, send_sem=send.at[slot], recv_sem=recv.at[slot],
            device_id=device, device_id_type=MESH)

    def far_row(side, group):
        return 2 * TOK + group * (2 * GROUP) + side * GROUP

    def g_group(side, group):
        return g.at[pl.ds(pl.multiple_of(far_row(side, group), 16), GROUP)]

    h_sent = []

    def send_far(count):
        while len(h_sent) < 2 * count:
            part = len(h_sent) // 2
            rows = pl.ds(part * PART, PART)
            group, inside = part * PART // GROUP, part * PART % GROUP
            to_far = remote(h_hbm.at[rows, own_cols],
                            h.at[pl.ds(far_row(0, group) + inside, PART)], H_FAR + part, far)
            to_farx = remote(h_hbm.at[rows, other_cols],
                             h.at[pl.ds(far_row(1, group) + inside, PART)], H_FARX + part, farx)
            to_far.start()
            to_farx.start()
            h_sent.extend([to_far, to_farx])

    stage0 = remote(g_hbm.at[pl.ds(pl.multiple_of(place * GROUP, GROUP), GROUP)],
                    g_group(0, place), STAGE0, cut)
    stage0.start()
    send_far(START_PARTS)
    g_sib = remote(g_hbm, g.at[pl.ds(TOK, TOK)], G_SIB, sibling)
    g_sib.start()
    h_sib = remote(h_hbm.at[:, other_cols], h.at[pl.ds(TOK, TOK)], H_SIB, sibling)
    h_sib.start()

    near = slice(0, 2 * TOK)
    rest = slice(2 * TOK, 4 * TOK)
    early = slice(2 * TOK, 2 * TOK + LATE)
    last = slice(2 * TOK + LATE, 4 * TOK)

    g_own.wait()
    g_sib.wait_recv()

    @step
    def out_local():
        keep(mo, *gram(g[near, :]))

    stage0.wait_recv()
    stage1 = [remote(g_group(0, place), g_group(0, place), STAGE1 + i, line[i]) for i in range(3)]
    for copy in stage1:
        copy.start()
    forwards = [remote(g_group(0, place), g_group(1, place), FORWARD, sibling)]
    forwards[0].start()
    send_far(PARTS)

    h_own.wait()
    h_sib.wait_recv()

    @step
    def in_local():
        keep(mi, *gram(h[near, :]))
        y[...] = mmt(h[near, :], g[near, :])

    for i in range(3):
        group = (place + 3 - i) % 4
        remote(g_group(0, group), g_group(0, group), STAGE1 + i, line[i]).wait_recv()
        forward = remote(g_group(0, group), g_group(1, group), FORWARD + 1 + i, sibling)
        forward.start()
        forwards.append(forward)
    sibling_place = zpos + core * (ypos - zpos)
    for i in range(4):
        group = (sibling_place + 4 - i) % 4
        remote(g_group(1, group), g_group(1, group), FORWARD + i, sibling).wait_recv()

    scale_tokens = 1.0 / (4 * TOK)

    so = 1.0 / jnp.sqrt(factor(mo, mob, g[rest, :], scale_tokens, OUT_DAMPING))

    mine = [(0, TOK)] + [(far_row(0, k), GROUP) for k in range(4)]

    def packed(ref):
        return jnp.concatenate([ref[a:a + n, :] for a, n in mine], axis=0)

    @step
    def out_two():
        two = residual(mo, mob, 2.0 * so, so * so)
        keep(p2, *two)
        keep_whole(p2b, *two)

    @step
    def corr_one():
        gm = packed(g)
        c1 = so * mm(gm, mob[...])
        cf[...] = c1
        zb[...] = (2.0 * gm.astype(F32) - c1).astype(BF16)

    @step
    def out_four():
        keep_whole(p4b, *residual(p2, p2b, 2.0, 1.0))

    @step
    def corr_two():
        c2 = 2.0 * cf[...] + mm(zb[...], p2b[...])
        cf[...] = c2
        zb[...] = (4.0 * packed(g).astype(F32) - c2).astype(BF16)

    corr = []

    @step
    def corr_three():
        c3 = ((2.0 * cf[...] + mm(zb[...], p4b[...])) * -0.125).astype(BF16)
        at = 0
        for a, n in mine:
            zc[a:a + n, :] = c3[at:at + n, :]
            at += n

    for i, (a, n) in enumerate(mine):
        copy = remote(zc.at[pl.ds(a, n)], zc.at[pl.ds(a + n, n)], CORR + i, sibling)
        copy.start()
        corr.append(copy)

    def take_far(lo, hi):
        for part in range(lo, hi):
            h_sent[2 * part].wait_recv()
            h_sent[2 * part + 1].wait_recv()

    early_parts = LATE // (2 * PART)
    take_far(0, early_parts)

    @step
    def in_early():
        add_gram(mi, h[early, :])
        y[...] += mmt(h[early, :], g[early, :])

    for copy in corr:
        copy.wait_recv()

    @step
    def right_early():
        y[...] += mmt(h[0:2 * TOK + LATE, :], zc[0:2 * TOK + LATE, :])

    take_far(early_parts, PARTS)
    damping_own.wait()
    block_damping = damping[hid * 2 + core]

    si = 1.0 / jnp.sqrt(factor(mi, mob, h[last, :], scale_tokens, block_damping))

    @step
    def right_last():
        r = y[...] + mmt(h[last, :], g[last, :]) + mmt(h[last, :], zc[last, :])
        y[...] = r
        ya[...] = r.astype(BF16)

    @step
    def in_two():
        two = residual(mi, mob, 2.0 * si, si * si)
        keep(p2, *two)
        keep_whole(p2b, *two)

    @step
    def apply_one():
        r = 2.0 * y[...] - si * mm(mob[...], ya[...])
        y[...] = r
        yb[...] = r.astype(BF16)

    @step
    def in_four():
        keep_whole(p4b, *residual(p2, p2b, 2.0, 1.0))

    @step
    def apply_two():
        r = 2.0 * y[...] - mm(p2b[...], yb[...])
        y[...] = r
        ya[...] = r.astype(BF16)

    final = 8.0 * si * so
    span = BLOCK // OUT_TILES

    def rows_of(owner, j):
        return u.at[pl.ds(pl.multiple_of(owner * BLOCK + j * span, span), span)]

    results = []
    for j in range(OUT_TILES):
        rs = slice(j * span, (j + 1) * span)

        @step
        def apply_three():
            r = 2.0 * y[rs, :] - mm(p4b[rs, :], ya[...])
            rows_of(core, j)[...] = (final * r).astype(BF16)

        results.append(remote(rows_of(core, j), rows_of(core, j), RESULT + j, sibling))
        results[j].start()

    for copy in [stage0, g_sib, h_sib] + h_sent + stage1 + forwards + corr + results:
        copy.wait_send()
    for j in range(OUT_TILES):
        remote(rows_of(1 - core, j), rows_of(1 - core, j), RESULT + j, sibling).wait_recv()


def local(hidden_acts, out_grads, damping):
    width = hidden_acts.shape[1]
    square = (BLOCK, BLOCK)
    hbm = pl.BlockSpec(memory_space=pl.ANY)
    return pl.pallas_call(
        kernel,
        name="kfac_step",
        out_shape=pltpu.VMEM((width, BLOCK), BF16),
        in_specs=[hbm, hbm, hbm],
        out_specs=pl.BlockSpec(memory_space=pltpu.VMEM),
        scratch_shapes=[
            pltpu.VMEM(square, BF16),
            pltpu.VMEM(square, BF16),
            pltpu.VMEM(square, F32),
            pltpu.VMEM(square, BF16),
            pltpu.VMEM(square, F32),
            pltpu.VMEM(square, BF16),
            pltpu.VMEM(square, BF16),
            pltpu.VMEM((BLOCK // 2, BLOCK), F32),
            pltpu.VMEM((BLOCK // 2, BLOCK), BF16),
            pltpu.VMEM(square, BF16),
            pltpu.VMEM(square, F32),
            pltpu.VMEM(square, F32),
            pltpu.VMEM(square, BF16),
            pltpu.VMEM(square, BF16),
            pltpu.SMEM((damping.shape[0],), F32),
            pltpu.SemaphoreType.DMA((N_REMOTE,)),
            pltpu.SemaphoreType.DMA((N_REMOTE,)),
            pltpu.SemaphoreType.DMA((3,)),
        ],
        compiler_params=pltpu.CompilerParams(
            collective_id=0, has_side_effects=True, vmem_limit_bytes=58 << 20
        ),
    )(hidden_acts, out_grads, damping)


def solution(mesh):
    return jax.shard_map(
        local,
        mesh=mesh,
        in_specs=(P("dp", "hid"), P("dp", None), P()),
        out_specs=P("hid", None),
        check_vma=False,
    )
```

```python
import jax
import jax.numpy as jnp
from jax import lax
from jax.experimental import pallas as pl
from jax.experimental.pallas import tpu as pltpu
from jax.sharding import PartitionSpec as P

BLOCK = 1024
OUT_DAMPING = 0.1
F32, BF16 = jnp.float32, jnp.bfloat16
MESH = pl.DeviceIdType.MESH
TOKENS_FIRST = (((0,), (0,)), ((), ()))

HALF = BLOCK // 2
TOP, LOW = slice(0, HALF), slice(HALF, BLOCK)

TOK = 256
GROUP = TOK // 4
PARTS = 8
PART = TOK // PARTS
LATE = 3 * GROUP * 2
OUT_ROWS = (512, 256, 256)

STAGE0, G_SIB, H_SIB, STAGE1, FORWARD, CORR, RESULT = 0, 1, 2, 3, 6, 10, 15
H_FAR = RESULT + len(OUT_ROWS)
H_FARX = H_FAR + PARTS
N_REMOTE = H_FARX + PARTS


def mm(a, b):
    return jnp.dot(a, b, preferred_element_type=F32)


def mmt(a, b):
    return lax.dot_general(a, b, TOKENS_FIRST, preferred_element_type=F32)


def total(m):
    rows, cols = m.shape
    return jnp.sum(jnp.sum((m * m).reshape(rows // 8, 8, cols), axis=0), keepdims=True)


def ridge(rows, cols, amount):
    row = lax.broadcasted_iota(jnp.int32, (rows, cols), 0)
    col = lax.broadcasted_iota(jnp.int32, (rows, cols), 1)
    return jnp.where(row == col, amount, 0.0)


def keep(ref, top, low):
    ref[TOP, :] = top
    ref[LOW, LOW] = low


def keep_whole(ref, top, low):
    keep(ref, top.astype(BF16), low.astype(BF16))
    ref[LOW, TOP] = top[:, LOW].astype(BF16).T


def gram(a):
    return mmt(a[:, TOP], a), mmt(a[:, LOW], a[:, LOW])


def add_gram(ref, a):
    top, low = gram(a)
    keep(ref, ref[TOP, :] + top, ref[LOW, LOW] + low)


def factor(ref, whole, a, scale, amount):
    top, low = gram(a)
    top = (ref[TOP, :] + top) * scale + ridge(HALF, BLOCK, amount)
    low = (ref[LOW, LOW] + low) * scale + ridge(HALF, HALF, amount)
    keep(ref, top, low)
    keep_whole(whole, top, low)
    return total(top[:, TOP]) + 2.0 * total(top[:, LOW]) + total(low)


def residual(ref, whole, linear, square):
    return (linear * ref[TOP, :] - square * mm(whole[TOP, :], whole[...]),
            linear * ref[LOW, LOW] - square * mm(whole[LOW, :], whole[:, LOW]))


def step(body):
    body()


def kernel(h_hbm, g_hbm, damping_hbm, u, h, ho, g, mo, mob, p2, p2b, p4b, cf, zb, zc,
           mi, y, ya, yb, damping, send, recv, here):
    hid, dp = lax.axis_index("hid"), lax.axis_index("dp")
    xlo, zpos, ypos = hid // 16, (hid // 4) % 4, hid % 4
    xhi, core = dp // 2, dp % 2

    place = ypos

    def beside(move):
        ny = (ypos + move) % 4
        return (xlo * 16 + zpos * 4 + ny, dp)

    sibling = (hid, xhi * 2 + 1 - core)
    far = (hid, (1 - xhi) * 2 + core)
    farx = (hid, (1 - xhi) * 2 + 1 - core)
    line = [beside(i) for i in range(1, 4)]

    own_cols = pl.ds(pl.multiple_of(core * BLOCK, BLOCK), BLOCK)
    other_cols = pl.ds(pl.multiple_of((1 - core) * BLOCK, BLOCK), BLOCK)
    g_own = pltpu.make_async_copy(g_hbm, g.at[pl.ds(0, TOK)], here.at[0])
    g_own.start()
    h_own = pltpu.make_async_copy(h_hbm.at[:, own_cols], h.at[pl.ds(0, TOK)], here.at[1])
    h_own.start()

    h_other = pltpu.make_async_copy(h_hbm.at[:, other_cols], ho, here.at[3])
    h_other.start()
    damping_own = pltpu.make_async_copy(damping_hbm, damping, here.at[2])
    damping_own.start()

    barrier = pltpu.get_barrier_semaphore()
    partners = [sibling, far, farx] + line
    for partner in partners:
        pl.semaphore_signal(barrier, 1, device_id=partner, device_id_type=MESH)
    pl.semaphore_wait(barrier, len(partners))

    def remote(src, dst, slot, device):
        return pltpu.make_async_remote_copy(
            src_ref=src, dst_ref=dst, send_sem=send.at[slot], recv_sem=recv.at[slot],
            device_id=device, device_id_type=MESH)

    def far_row(side, group):
        return 2 * TOK + group * (2 * GROUP) + side * GROUP

    def g_group(side, group):
        return g.at[pl.ds(pl.multiple_of(far_row(side, group), 16), GROUP)]

    h_sent = []

    def send_far(count):
        while len(h_sent) < 2 * count:
            part = len(h_sent) // 2
            rows = pl.ds(part * PART, PART)
            group, inside = part * PART // GROUP, part * PART % GROUP
            to_far = remote(h.at[rows],
                            h.at[pl.ds(far_row(0, group) + inside, PART)], H_FAR + part, far)
            to_farx = remote(ho.at[rows],
                             h.at[pl.ds(far_row(1, group) + inside, PART)], H_FARX + part, farx)
            to_far.start()
            to_farx.start()
            h_sent.extend([to_far, to_farx])

    stage0 = remote(g_hbm.at[pl.ds(pl.multiple_of(place * GROUP, GROUP), GROUP)],
                    g_group(0, place), STAGE0, far)
    stage0.start()
    h_own.wait()
    h_other.wait()
    send_far(PARTS)
    g_sib = remote(g_hbm, g.at[pl.ds(TOK, TOK)], G_SIB, sibling)
    g_sib.start()
    h_sib = remote(ho, h.at[pl.ds(TOK, TOK)], H_SIB, sibling)
    h_sib.start()

    near = slice(0, 2 * TOK)
    rest = slice(2 * TOK, 4 * TOK)
    early = slice(2 * TOK, 2 * TOK + LATE)
    last = slice(2 * TOK + LATE, 4 * TOK)

    g_own.wait()
    g_sib.wait_recv()

    @step
    def out_local():
        keep(mo, *gram(g[near, :]))

    stage0.wait_recv()
    stage1 = [remote(g_group(0, place), g_group(0, place), STAGE1 + i, line[i]) for i in range(3)]
    for copy in stage1:
        copy.start()
    forwards = [remote(g_group(0, place), g_group(1, place), FORWARD, sibling)]
    forwards[0].start()
    h_sib.wait_recv()

    @step
    def in_local():
        keep(mi, *gram(h[near, :]))
        y[...] = mmt(h[near, :], g[near, :])

    for i in range(3):
        group = (place + 3 - i) % 4
        remote(g_group(0, group), g_group(0, group), STAGE1 + i, line[i]).wait_recv()
        forward = remote(g_group(0, group), g_group(1, group), FORWARD + 1 + i, sibling)
        forward.start()
        forwards.append(forward)
    for i in range(4):
        group = (place + 4 - i) % 4
        remote(g_group(1, group), g_group(1, group), FORWARD + i, sibling).wait_recv()

    scale_tokens = 1.0 / (4 * TOK)

    so = 1.0 / jnp.sqrt(factor(mo, mob, g[rest, :], scale_tokens, OUT_DAMPING))

    mine = [(0, TOK)] + [(far_row(0, k), GROUP) for k in range(4)]

    def packed(ref):
        return jnp.concatenate([ref[a:a + n, :] for a, n in mine], axis=0)

    @step
    def out_two():
        two = residual(mo, mob, 2.0 * so, so * so)
        keep(p2, *two)
        keep_whole(p2b, *two)

    @step
    def corr_one():
        gm = packed(g)
        c1 = so * mm(gm, mob[...])
        cf[...] = c1
        zb[...] = (2.0 * gm.astype(F32) - c1).astype(BF16)

    @step
    def out_four():
        keep_whole(p4b, *residual(p2, p2b, 2.0, 1.0))

    @step
    def corr_two():
        c2 = 2.0 * cf[...] + mm(zb[...], p2b[...])
        cf[...] = c2
        zb[...] = (4.0 * packed(g).astype(F32) - c2).astype(BF16)

    corr = []

    @step
    def corr_three():
        c3 = ((2.0 * cf[...] + mm(zb[...], p4b[...])) * -0.125).astype(BF16)
        at = 0
        for a, n in mine:
            zc[a:a + n, :] = c3[at:at + n, :]
            at += n

    for i, (a, n) in enumerate(mine):
        copy = remote(zc.at[pl.ds(a, n)], zc.at[pl.ds(a + n, n)], CORR + i, sibling)
        copy.start()
        corr.append(copy)

    def take_far(lo, hi):
        for part in range(lo, hi):
            h_sent[2 * part].wait_recv()
            h_sent[2 * part + 1].wait_recv()

    early_parts = LATE // (2 * PART)
    take_far(0, early_parts)

    @step
    def in_early():
        add_gram(mi, h[early, :])
        y[...] += mmt(h[early, :], g[early, :])

    for copy in corr:
        copy.wait_recv()

    @step
    def right_early():
        y[...] += mmt(h[0:2 * TOK + LATE, :], zc[0:2 * TOK + LATE, :])

    take_far(early_parts, PARTS)
    damping_own.wait()
    block_damping = damping[hid * 2 + core]

    si = 1.0 / jnp.sqrt(factor(mi, mob, h[last, :], scale_tokens, block_damping))

    @step
    def right_last():
        r = y[...] + mmt(h[last, :], g[last, :]) + mmt(h[last, :], zc[last, :])
        y[...] = r
        ya[...] = r.astype(BF16)

    @step
    def in_two():
        two = residual(mi, mob, 2.0 * si, si * si)
        keep(p2, *two)
        keep_whole(p2b, *two)

    @step
    def apply_one():
        r = 2.0 * y[...] - si * mm(mob[...], ya[...])
        y[...] = r
        yb[...] = r.astype(BF16)

    @step
    def in_four():
        keep_whole(p4b, *residual(p2, p2b, 2.0, 1.0))

    @step
    def apply_two():
        r = 2.0 * y[...] - mm(p2b[...], yb[...])
        y[...] = r
        ya[...] = r.astype(BF16)

    final = 8.0 * si * so

    def rows_of(owner, start, size):
        return u.at[pl.ds(pl.multiple_of(owner * BLOCK + start, 256), size)]

    results, start = [], 0
    for j, size in enumerate(OUT_ROWS):
        rs = slice(start, start + size)

        @step
        def apply_three():
            r = 2.0 * y[rs, :] - mm(p4b[rs, :], ya[...])
            rows_of(core, start, size)[...] = (final * r).astype(BF16)

        results.append(remote(rows_of(core, start, size), rows_of(core, start, size),
                              RESULT + j, sibling))
        results[j].start()
        start += size

    for copy in [stage0, g_sib, h_sib] + h_sent + stage1 + forwards + corr + results:
        copy.wait_send()
    start = 0
    for j, size in enumerate(OUT_ROWS):
        came = rows_of(1 - core, start, size)
        remote(came, came, RESULT + j, sibling).wait_recv()
        start += size


def local(hidden_acts, out_grads, damping):
    width = hidden_acts.shape[1]
    square = (BLOCK, BLOCK)
    hbm = pl.BlockSpec(memory_space=pl.ANY)
    return pl.pallas_call(
        kernel,
        name="kfac_step",
        out_shape=pltpu.VMEM((width, BLOCK), BF16),
        in_specs=[hbm, hbm, hbm],
        out_specs=pl.BlockSpec(memory_space=pltpu.VMEM),
        scratch_shapes=[
            pltpu.VMEM(square, BF16),
            pltpu.VMEM((TOK, BLOCK), BF16),
            pltpu.VMEM(square, BF16),
            pltpu.VMEM(square, F32),
            pltpu.VMEM(square, BF16),
            pltpu.VMEM(square, F32),
            pltpu.VMEM(square, BF16),
            pltpu.VMEM(square, BF16),
            pltpu.VMEM((BLOCK // 2, BLOCK), F32),
            pltpu.VMEM((BLOCK // 2, BLOCK), BF16),
            pltpu.VMEM(square, BF16),
            pltpu.VMEM(square, F32),
            pltpu.VMEM(square, F32),
            pltpu.VMEM(square, BF16),
            pltpu.VMEM(square, BF16),
            pltpu.SMEM((damping.shape[0],), F32),
            pltpu.SemaphoreType.DMA((N_REMOTE,)),
            pltpu.SemaphoreType.DMA((N_REMOTE,)),
            pltpu.SemaphoreType.DMA((4,)),
        ],
        compiler_params=pltpu.CompilerParams(
            collective_id=0, has_side_effects=True, vmem_limit_bytes=58 << 20
        ),
    )(hidden_acts, out_grads, damping)


def solution(mesh):
    return jax.shard_map(
        local,
        mesh=mesh,
        in_specs=(P("dp", "hid"), P("dp", None), P()),
        out_specs=P("hid", None),
        check_vma=False,
    )
```

```python
import jax
import jax.numpy as jnp
from jax import lax
from jax.experimental import pallas as pl
from jax.experimental.pallas import tpu as pltpu
from jax.sharding import PartitionSpec as P

BLOCK = 1024
OUT_DAMPING = 0.1
F32, BF16 = jnp.float32, jnp.bfloat16
MESH = pl.DeviceIdType.MESH
TOKENS_FIRST = (((0,), (0,)), ((), ()))

HALF = BLOCK // 2
TOP, LOW = slice(0, HALF), slice(HALF, BLOCK)

TOK = 256
GROUP = TOK // 4
PARTS = 8
PART = TOK // PARTS
LATE = 3 * GROUP * 2
OUT_ROWS = (512, 256, 128, 128)

STAGE0, G_SIB, H_SIB, STAGE1, FORWARD, CORR, RESULT = 0, 1, 2, 3, 6, 10, 15
H_FAR = RESULT + len(OUT_ROWS)
H_FARX = H_FAR + PARTS
N_REMOTE = H_FARX + PARTS


def mm(a, b):
    return jnp.dot(a, b, preferred_element_type=F32)


def mmt(a, b):
    return lax.dot_general(a, b, TOKENS_FIRST, preferred_element_type=F32)


def total(m):
    rows, cols = m.shape
    return jnp.sum(jnp.sum((m * m).reshape(rows // 8, 8, cols), axis=0), keepdims=True)


def ridge(rows, cols, amount):
    row = lax.broadcasted_iota(jnp.int32, (rows, cols), 0)
    col = lax.broadcasted_iota(jnp.int32, (rows, cols), 1)
    return jnp.where(row == col, amount, 0.0)


def keep(ref, top, low):
    ref[TOP, :] = top
    ref[LOW, LOW] = low


def keep_whole(ref, top, low):
    keep(ref, top.astype(BF16), low.astype(BF16))
    ref[LOW, TOP] = top[:, LOW].astype(BF16).T


def gram(a):
    return mmt(a[:, TOP], a), mmt(a[:, LOW], a[:, LOW])


def add_gram(ref, a):
    top, low = gram(a)
    keep(ref, ref[TOP, :] + top, ref[LOW, LOW] + low)


def factor(ref, whole, a, scale, amount):
    top, low = gram(a)
    top = (ref[TOP, :] + top) * scale + ridge(HALF, BLOCK, amount)
    low = (ref[LOW, LOW] + low) * scale + ridge(HALF, HALF, amount)
    keep(ref, top, low)
    keep_whole(whole, top, low)
    return total(top[:, TOP]) + 2.0 * total(top[:, LOW]) + total(low)


def residual(ref, whole, linear, square):
    return (linear * ref[TOP, :] - square * mm(whole[TOP, :], whole[...]),
            linear * ref[LOW, LOW] - square * mm(whole[LOW, :], whole[:, LOW]))


def step(body):
    body()


def kernel(h_hbm, g_hbm, damping_hbm, u, h, ho, g, mo, mob, p2, p2b, p4b, cf, zb, zc,
           mi, y, ya, yb, damping, send, recv, here):
    hid, dp = lax.axis_index("hid"), lax.axis_index("dp")
    xlo, zpos, ypos = hid // 16, (hid // 4) % 4, hid % 4
    xhi, core = dp // 2, dp % 2

    place = ypos

    def beside(move):
        ny = (ypos + move) % 4
        return (xlo * 16 + zpos * 4 + ny, dp)

    sibling = (hid, xhi * 2 + 1 - core)
    far = (hid, (1 - xhi) * 2 + core)
    farx = (hid, (1 - xhi) * 2 + 1 - core)
    line = [beside(i) for i in range(1, 4)]

    own_cols = pl.ds(pl.multiple_of(core * BLOCK, BLOCK), BLOCK)
    other_cols = pl.ds(pl.multiple_of((1 - core) * BLOCK, BLOCK), BLOCK)
    g_own = pltpu.make_async_copy(g_hbm, g.at[pl.ds(0, TOK)], here.at[0])
    g_own.start()
    h_own = pltpu.make_async_copy(h_hbm.at[:, own_cols], h.at[pl.ds(0, TOK)], here.at[1])
    h_own.start()

    h_other = pltpu.make_async_copy(h_hbm.at[:, other_cols], ho, here.at[3])
    h_other.start()
    damping_own = pltpu.make_async_copy(damping_hbm, damping, here.at[2])
    damping_own.start()

    barrier = pltpu.get_barrier_semaphore()
    partners = [sibling, far, farx] + line
    for partner in partners:
        pl.semaphore_signal(barrier, 1, device_id=partner, device_id_type=MESH)
    pl.semaphore_wait(barrier, len(partners))

    def remote(src, dst, slot, device):
        return pltpu.make_async_remote_copy(
            src_ref=src, dst_ref=dst, send_sem=send.at[slot], recv_sem=recv.at[slot],
            device_id=device, device_id_type=MESH)

    def far_row(side, group):
        return 2 * TOK + group * (2 * GROUP) + side * GROUP

    def g_group(side, group):
        return g.at[pl.ds(pl.multiple_of(far_row(side, group), 16), GROUP)]

    h_sent = []

    def send_far(count):
        while len(h_sent) < 2 * count:
            part = len(h_sent) // 2
            rows = pl.ds(part * PART, PART)
            group, inside = part * PART // GROUP, part * PART % GROUP
            to_far = remote(h.at[rows],
                            h.at[pl.ds(far_row(0, group) + inside, PART)], H_FAR + part, far)
            to_farx = remote(ho.at[rows],
                             h.at[pl.ds(far_row(1, group) + inside, PART)], H_FARX + part, farx)
            to_far.start()
            to_farx.start()
            h_sent.extend([to_far, to_farx])

    stage0 = remote(g_hbm.at[pl.ds(pl.multiple_of(place * GROUP, GROUP), GROUP)],
                    g_group(0, place), STAGE0, far)
    stage0.start()
    h_own.wait()
    h_other.wait()
    send_far(PARTS)
    g_sib = remote(g_hbm, g.at[pl.ds(TOK, TOK)], G_SIB, sibling)
    g_sib.start()
    h_sib = remote(ho, h.at[pl.ds(TOK, TOK)], H_SIB, sibling)
    h_sib.start()

    near = slice(0, 2 * TOK)
    rest = slice(2 * TOK, 4 * TOK)
    half = slice(2 * TOK, 3 * TOK)
    third = slice(3 * TOK, 2 * TOK + LATE)
    last = slice(2 * TOK + LATE, 4 * TOK)

    stage0.wait_recv()
    stage1 = [remote(g_group(0, place), g_group(0, place), STAGE1 + i, line[i]) for i in range(3)]
    for copy in stage1:
        copy.start()
    forwards = [remote(g_group(0, place), g_group(1, place), FORWARD, sibling)]
    forwards[0].start()
    g_own.wait()
    g_sib.wait_recv()

    @step
    def out_local():
        keep(mo, *gram(g[near, :]))

    h_sib.wait_recv()

    @step
    def in_local():
        keep(mi, *gram(h[near, :]))
        y[...] = mmt(h[near, :], g[near, :])

    for i in range(3):
        group = (place + 3 - i) % 4
        remote(g_group(0, group), g_group(0, group), STAGE1 + i, line[i]).wait_recv()
        forward = remote(g_group(0, group), g_group(1, group), FORWARD + 1 + i, sibling)
        forward.start()
        forwards.append(forward)
    for i in range(4):
        group = (place + 4 - i) % 4
        remote(g_group(1, group), g_group(1, group), FORWARD + i, sibling).wait_recv()

    scale_tokens = 1.0 / (4 * TOK)

    so = 1.0 / jnp.sqrt(factor(mo, mob, g[rest, :], scale_tokens, OUT_DAMPING))

    mine = [(0, TOK)] + [(far_row(0, k), GROUP) for k in range(4)]

    def packed(ref):
        return jnp.concatenate([ref[a:a + n, :] for a, n in mine], axis=0)

    @step
    def out_two():
        two = residual(mo, mob, 2.0 * so, so * so)
        keep(p2, *two)
        keep_whole(p2b, *two)

    @step
    def corr_one():
        gm = packed(g)
        c1 = so * mm(gm, mob[...])
        cf[...] = c1
        zb[...] = (2.0 * gm.astype(F32) - c1).astype(BF16)

    @step
    def out_four():
        keep_whole(p4b, *residual(p2, p2b, 2.0, 1.0))

    @step
    def corr_two():
        c2 = 2.0 * cf[...] + mm(zb[...], p2b[...])
        cf[...] = c2
        zb[...] = (4.0 * packed(g).astype(F32) - c2).astype(BF16)

    corr = []

    def take_far(lo, hi):
        for part in range(lo, hi):
            h_sent[2 * part].wait_recv()
            h_sent[2 * part + 1].wait_recv()

    take_far(0, PARTS // 2)

    @step
    def in_half():
        add_gram(mi, h[half, :])
        y[...] += mmt(h[half, :], g[half, :])

    @step
    def corr_three():
        c3 = ((2.0 * cf[...] + mm(zb[...], p4b[...])) * -0.125).astype(BF16)
        at = 0
        for a, n in mine:
            zc[a:a + n, :] = c3[at:at + n, :]
            at += n

    for i, (a, n) in enumerate(mine):
        copy = remote(zc.at[pl.ds(a, n)], zc.at[pl.ds(a + n, n)], CORR + i, sibling)
        copy.start()
        corr.append(copy)

    early_parts = LATE // (2 * PART)
    take_far(PARTS // 2, early_parts)

    @step
    def in_early():
        add_gram(mi, h[third, :])
        y[...] += mmt(h[third, :], g[third, :])

    for copy in corr:
        copy.wait_recv()

    @step
    def right_early():
        y[...] += mmt(h[0:2 * TOK + LATE, :], zc[0:2 * TOK + LATE, :])

    take_far(early_parts, PARTS)
    damping_own.wait()
    block_damping = damping[hid * 2 + core]

    si = 1.0 / jnp.sqrt(factor(mi, mob, h[last, :], scale_tokens, block_damping))

    @step
    def right_last():
        r = y[...] + mmt(h[last, :], g[last, :]) + mmt(h[last, :], zc[last, :])
        y[...] = r
        ya[...] = r.astype(BF16)

    @step
    def in_two():
        two = residual(mi, mob, 2.0 * si, si * si)
        keep(p2, *two)
        keep_whole(p2b, *two)

    @step
    def apply_one():
        r = 2.0 * y[...] - si * mm(mob[...], ya[...])
        y[...] = r
        yb[...] = r.astype(BF16)

    @step
    def in_four():
        keep_whole(p4b, *residual(p2, p2b, 2.0, 1.0))

    @step
    def apply_two():
        r = 2.0 * y[...] - mm(p2b[...], yb[...])
        y[...] = r
        ya[...] = r.astype(BF16)

    final = 8.0 * si * so

    def rows_of(owner, start, size):
        return u.at[pl.ds(pl.multiple_of(owner * BLOCK + start, 128), size)]

    results, start = [], 0
    for j, size in enumerate(OUT_ROWS):
        rs = slice(start, start + size)

        @step
        def apply_three():
            r = 2.0 * y[rs, :] - mm(p4b[rs, :], ya[...])
            rows_of(core, start, size)[...] = (final * r).astype(BF16)

        results.append(remote(rows_of(core, start, size), rows_of(core, start, size),
                              RESULT + j, sibling))
        results[j].start()
        start += size

    for copy in [stage0, g_sib, h_sib] + h_sent + stage1 + forwards + corr + results:
        copy.wait_send()
    start = 0
    for j, size in enumerate(OUT_ROWS):
        came = rows_of(1 - core, start, size)
        remote(came, came, RESULT + j, sibling).wait_recv()
        start += size


def local(hidden_acts, out_grads, damping):
    width = hidden_acts.shape[1]
    square = (BLOCK, BLOCK)
    hbm = pl.BlockSpec(memory_space=pl.ANY)
    return pl.pallas_call(
        kernel,
        name="kfac_step",
        out_shape=pltpu.VMEM((width, BLOCK), BF16),
        in_specs=[hbm, hbm, hbm],
        out_specs=pl.BlockSpec(memory_space=pltpu.VMEM),
        scratch_shapes=[
            pltpu.VMEM(square, BF16),
            pltpu.VMEM((TOK, BLOCK), BF16),
            pltpu.VMEM(square, BF16),
            pltpu.VMEM(square, F32),
            pltpu.VMEM(square, BF16),
            pltpu.VMEM(square, F32),
            pltpu.VMEM(square, BF16),
            pltpu.VMEM(square, BF16),
            pltpu.VMEM((BLOCK // 2, BLOCK), F32),
            pltpu.VMEM((BLOCK // 2, BLOCK), BF16),
            pltpu.VMEM(square, BF16),
            pltpu.VMEM(square, F32),
            pltpu.VMEM(square, F32),
            pltpu.VMEM(square, BF16),
            pltpu.VMEM(square, BF16),
            pltpu.SMEM((damping.shape[0],), F32),
            pltpu.SemaphoreType.DMA((N_REMOTE,)),
            pltpu.SemaphoreType.DMA((N_REMOTE,)),
            pltpu.SemaphoreType.DMA((4,)),
        ],
        compiler_params=pltpu.CompilerParams(
            collective_id=0, has_side_effects=True, vmem_limit_bytes=58 << 20
        ),
    )(hidden_acts, out_grads, damping)


def solution(mesh):
    return jax.shard_map(
        local,
        mesh=mesh,
        in_specs=(P("dp", "hid"), P("dp", None), P()),
        out_specs=P("hid", None),
        check_vma=False,
    )
```
